512 devices in a mesh: row: 32 (over x, y), col: 16 (over z, core).
Axes of the slice: x: 4, y: 8, z: 8, core: 2. Of those that a mesh axis runs over, the one named last changes fastest.
Arguments:
- features: bfloat16 [32, 2048, 256], P('row', 'col'), may hold values from -6 to 6
- weight: bfloat16 [256, 256], replicated, may hold values from -0.375 to 0.375
- tile_values: bfloat16 [32, 16, 48, 128, 128], P('row', 'col'), may hold values from -0.109375 to 0.109375
- tile_places: int32 [32, 16, 2, 48], P('row', 'col'), may hold values from 0 to 31, as said below
- tile_count: int32 [32, 16], P('row', 'col'), may hold values from 1 to 48, as said below
- upstream: bfloat16 [16, 4096, 256], P('col', 'row'), may hold values from -6 to 6
Outputs:
- activations: bfloat16 [16, 4096, 256], P('col', 'row')
- grad_features: bfloat16 [32, 2048, 256], P('row', 'col')
- grad_weight: float32 [256, 256], replicated
The draws below stay inside these ranges and needn't reach their ends.
Inputs may be any that keep to these rules, and one draw needn't show every extreme that they name: `tile_places`: [r, c, 0, s] is a tile row, below 32, and [r, c, 1, s] a tile column, below 16, of slot s of block (r, c); positions may repeat, and repeated tiles add. `tile_count`: slots at or beyond this number hold no tile; some block is full.
All inputs are finite; a program needn't handle non-finite values.
Results may differ from the reference program's by a relative error of at most 0.02.
Values may be sent and summed in bfloat16 or wider, within the bound.
No kernel may reach another device: no remote copies, remote signals or barrier semaphores. Data moves between devices by JAX's collectives and lax.ppermute only.
A program may use at most 64 MiB of HBM per device.

```python
import jax
import jax.numpy as jnp
from jax import lax

F = 256
FO = 256
TILE = 128
SUB = 128
TMAX = 48
NODES = 65536
TROWS = 32
TCOLS = 16
N_ROW = 32
N_COL = 16


def draw_tile_places(key, part):
    row_key, col_key, pick_key, other_key = jax.random.split(key, 4)
    tile_rows = jax.random.randint(row_key, (N_ROW, N_COL, TMAX), 0, TROWS)
    tile_cols = jax.random.randint(col_key, (N_ROW, N_COL, TMAX), 0, TCOLS)
    slot_first = jax.random.randint(pick_key, (N_ROW, N_COL, 1), 0, TMAX)
    slot_second = jax.random.randint(other_key, (N_ROW, N_COL, 1), 0, TMAX)
    slot_ids = jnp.arange(TMAX, dtype=jnp.int32)
    tile_rows = jnp.where(slot_ids == slot_first, TROWS - 1, tile_rows)
    tile_cols = jnp.where(slot_ids == slot_second, TCOLS - 1, tile_cols)
    return jnp.stack([tile_rows, tile_cols], axis=2).astype(jnp.int32)


def draw_tile_count(key, part):
    hub_key, light_key, pick_key = jax.random.split(key, 3)
    hub_flags = jax.random.randint(hub_key, (N_ROW, N_COL), 0, 4) == 0
    light_counts = jax.random.randint(light_key, (N_ROW, N_COL), max(1, TMAX // 8), TMAX // 2 + 1)
    counts = jnp.where(hub_flags, TMAX, light_counts)
    chosen = jax.random.randint(pick_key, (), 0, N_ROW * N_COL)
    flat_counts = jnp.where(jnp.arange(N_ROW * N_COL) == chosen, TMAX, counts.reshape(-1))
    return flat_counts.reshape(N_ROW, N_COL).astype(jnp.int32)


def steps_of(key, extent, cuts, smallest, largest):
    def one(axis_at, blocks):
        draws = jax.random.uniform(jax.random.fold_in(jax.random.fold_in(key, 6), axis_at), (blocks,), jnp.float32, smallest / len(cuts), largest / len(cuts))
        return jnp.repeat(jnp.exp(draws), extent[axis_at] // blocks).reshape((-1,) + (1,) * (len(extent) - axis_at - 1))

    loudness = one(*cuts[0])
    for cut in cuts[1:]:
        loudness = loudness * one(*cut)
    return loudness


def normal_values(key, extent, width, reach, cuts=(), kind=jnp.bfloat16):
    drawn = jax.random.normal(key, extent, jnp.float32) * width
    if len(cuts) > 0:
        drawn = steps_of(key, extent, cuts, -0.22, 0.18) * drawn
    return jnp.clip(drawn, min=-reach, max=reach).astype(kind)


def setup_inputs(seed: int = 0) -> dict:
    key_list = jax.random.split(jax.random.key(seed), 7)
    return {
        "features": normal_values(key_list[0], (N_ROW, SUB * N_COL, F), 1.0, 6.0, ((0, 32), (1, 16))),
        "weight": normal_values(key_list[1], (F, FO), F ** -0.5, 0.375),
        "tile_values": normal_values(key_list[2], (N_ROW, N_COL, TMAX, TILE, TILE), (TMAX * TILE * TILE // (2 * SUB)) ** -0.5, 0.109375, ((0, 32), (1, 16))),
        "tile_places": draw_tile_places(jax.random.fold_in(key_list[6], 71), 0),
        "tile_count": draw_tile_count(jax.random.fold_in(key_list[6], 71), 0),
        "upstream": normal_values(key_list[5], (N_COL, SUB * N_ROW, FO), 1.0, 6.0, ((0, 16), (1, 32))),
    }


def rounded(values):
    return lax.optimization_barrier(values.astype(jnp.bfloat16)).astype(jnp.float32)


def block_product(tile_set, places, live_count, source_tiles, transpose, dest_tiles):
    slot_ids = jnp.arange(TMAX, dtype=jnp.int32)
    live_mask = slot_ids < live_count
    if transpose:
        take_index = places[0]
        put_index = places[1]
        operand = jnp.swapaxes(tile_set.astype(jnp.float32), 1, 2)
    else:
        take_index = places[1]
        put_index = places[0]
        operand = tile_set.astype(jnp.float32)
    slab_rows = source_tiles[take_index].astype(jnp.float32)
    products = jnp.einsum("sik,skf->sif", operand, slab_rows)
    products = jnp.where(live_mask[:, None, None], products, jnp.float32(0.0))
    running = jnp.zeros((dest_tiles, TILE, FO), jnp.float32).at[put_index].add(products)
    return running.reshape(dest_tiles * TILE, FO)


def reference(features, weight, tile_values, tile_places, tile_count, upstream):
    flat_features = features.reshape(NODES, F)
    projected = jnp.dot(flat_features, weight, preferred_element_type=jnp.float32).astype(jnp.bfloat16)
    proj_tiles = projected.reshape(N_ROW, TCOLS, TILE, FO)

    def forward_column(column):
        def add_device(running, row_pos):
            partial_value = block_product(tile_values[row_pos, column], tile_places[row_pos, column],
                                    tile_count[row_pos, column], proj_tiles[row_pos], False, TROWS)
            return running + rounded(partial_value), None
        total_sum, unused = lax.scan(add_device, jnp.zeros((TROWS * TILE, FO), jnp.float32),
                                     jnp.arange(N_ROW, dtype=jnp.int32))
        return total_sum

    pre_act = lax.map(forward_column, jnp.arange(N_COL, dtype=jnp.int32))
    sigma = jax.nn.sigmoid(pre_act)
    activations = (pre_act * sigma).astype(jnp.bfloat16)
    slope = (upstream.astype(jnp.float32) * sigma * (1.0 + pre_act * (1.0 - sigma))).astype(jnp.bfloat16)
    slope_tiles = slope.reshape(N_COL, TROWS, TILE, FO)

    def backward_row(row_pos):
        def add_device(running, column):
            partial_value = block_product(tile_values[row_pos, column], tile_places[row_pos, column],
                                    tile_count[row_pos, column], slope_tiles[column], True, TCOLS)
            return running + rounded(partial_value), None
        total_sum, unused = lax.scan(add_device, jnp.zeros((TCOLS * TILE, FO), jnp.float32),
                                     jnp.arange(N_COL, dtype=jnp.int32))
        return total_sum

    grad_proj = lax.map(backward_row, jnp.arange(N_ROW, dtype=jnp.int32)).astype(jnp.bfloat16)
    flat_grad = grad_proj.reshape(NODES, FO)
    grad_features = jnp.dot(flat_grad, weight.T, preferred_element_type=jnp.float32).astype(jnp.bfloat16)
    grad_weight = jnp.dot(flat_features.T, flat_grad, preferred_element_type=jnp.float32)
    return activations, grad_features.reshape(N_ROW, SUB * N_COL, F), grad_weight
```

```python
import jax
import jax.numpy as jnp
from jax import lax
from jax.experimental import pallas as pl
from jax.experimental.pallas import tpu as pltpu
from jax.sharding import Mesh, PartitionSpec as P

BF = jnp.bfloat16
F32 = jnp.float32
VM = pl.BlockSpec(memory_space=pltpu.VMEM)
SM = pl.BlockSpec(memory_space=pltpu.SMEM)
T = 128
GROUP = 4


def call(kernel, outs, in_specs, *args, scratch=(), limit=24 << 20):
    return pl.pallas_call(
        kernel,
        out_shape=outs,
        in_specs=in_specs,
        out_specs=jax.tree.map(lambda _: VM, outs),
        scratch_shapes=scratch,
        compiler_params=pltpu.CompilerParams(vmem_limit_bytes=limit),
    )(*args)


def shape(dims, kind=BF):
    return jax.ShapeDtypeStruct(dims, kind)


def block_products(count_ref, tiles_ref, acc_ref, put, load, contract):
    slots = tiles_ref.shape[0]
    acc_ref[...] = jnp.zeros_like(acc_ref)
    count = count_ref[0, 0]

    def group(g, carry):
        products = []
        for k in range(GROUP):
            s = jnp.minimum(g * GROUP + k, slots - 1)
            product = lax.dot_general(
                tiles_ref[s], load(s), (((contract,), (0,)), ((), ())), preferred_element_type=F32
            )
            products.append((put(s), jnp.where(g * GROUP + k < count, product, 0.0)))
        for at, product in products:
            acc_ref[at] += product
        return carry

    lax.fori_loop(0, (count + GROUP - 1) // GROUP, group, 0)


def forward_kernel(places, count, tiles, own, other, out, acc):
    core = lax.axis_index("c")

    def load(s):
        col = places[1, s]
        z = col // 2
        return jnp.where(col % 2 == core, own[z], other[z])

    block_products(count, tiles, acc, lambda s: places[0, s], load, 1)
    out[...] = acc[...].astype(BF).reshape(out.shape)


def sum_kernel(parts, out):
    total = parts[0].astype(F32)
    for k in range(1, parts.shape[0]):
        total += parts[k].astype(F32)
    out[...] = total.astype(BF)


def node_kernel(parts, weight, upstream, act, send):
    agg = parts[0].astype(F32)
    for k in range(1, parts.shape[0]):
        agg += parts[k].astype(F32)
    agg = agg.astype(BF)
    pre = jnp.dot(agg, weight[...], preferred_element_type=F32)
    sigma = jax.nn.sigmoid(pre)
    act[...] = (pre * sigma).astype(BF)
    slope = (upstream[...].astype(F32) * sigma * (1.0 + pre * (1.0 - sigma))).astype(BF)
    back = lax.dot_general(
        slope, weight[...], (((1,), (1,)), ((), ())), preferred_element_type=F32
    ).astype(BF)
    term = lax.dot_general(agg, slope, (((0,), (0,)), ((), ())), preferred_element_type=F32)
    for y in range(8):
        send[y, :T] = back
        rows = [term[x * 64 + y * 8 : x * 64 + y * 8 + 8] for x in range(4)]
        send[y, T:] = jnp.concatenate(rows, 0).astype(BF)


def spread_kernel(got, send):
    term = got[0, T:].astype(F32)
    for k in range(1, 8):
        term += got[k, T:].astype(F32)
    high = term.astype(BF).astype(F32)
    low = term - high
    for x in range(4):
        for y in range(8):
            send[x, y * T : (y + 1) * T] = got[y, :T]
        rows = slice(x * 8, x * 8 + 8)
        send[x, 8 * T :] = jnp.concatenate([high[rows], low[rows]], 0).astype(BF)


def backward_kernel(places, count, tiles, got, keep, send, term, acc):
    core = lax.axis_index("c")

    def load(s):
        row = places[0, s]
        return got[row // 8, pl.ds(pl.multiple_of((row % 8) * T, T), T)]

    block_products(count, tiles, acc, lambda s: places[1, s], load, 0)
    for z in range(8):
        keep[z] = acc[2 * z + core].astype(BF)
        send[z * T : (z + 1) * T] = acc[2 * z + 1 - core].astype(BF)
    total = got[0, 8 * T :].astype(F32)
    for k in range(1, 4):
        total += got[k, 8 * T :].astype(F32)
    total = total[:8] + total[8:]
    term[...] = total
    high = total.astype(BF).astype(F32)
    send[8 * T :] = jnp.concatenate([high, total - high], 0).astype(BF)


def join_kernel(keep, got, term, send):
    other = got[8 * T :].astype(F32)
    total = term[...] + (other[:8] + other[8:])
    high = total.astype(BF).astype(F32)
    both = jnp.concatenate([high, total - high], 0).astype(BF)
    for z in range(8):
        send[z, :T] = (keep[z].astype(F32) + got[z * T : (z + 1) * T].astype(F32)).astype(BF)
        send[z, T:] = both


def last_kernel(got, grad, term):
    total = got[0].astype(F32)
    for k in range(1, 8):
        total += got[k].astype(F32)
    grad[...] = total[:T].astype(BF)
    rows = total[T : T + 8] + total[T + 8 :]
    for k in range(32):
        term[k] = rows


def per_device(features, weight, tile_values, tile_places, tile_count, upstream):
    own_rows = features[0]
    tiles = tile_values[0, 0]
    places = tile_places[0, 0]
    swap = [(0, 1), (1, 0)]

    own = lax.all_to_all(jnp.broadcast_to(own_rows, (8, T, 256)), "z", 0, 0)
    other = lax.ppermute(own, "c", swap)
    partial = call(
        forward_kernel, shape((4, 8 * T, 256)), [SM, SM, VM, VM, VM],
        places, tile_count, tiles, own, other, scratch=[pltpu.VMEM((32, T, 256), F32)],
    )
    parts = lax.all_to_all(partial, "x", 0, 0)
    parts = call(sum_kernel, shape((8 * T, 256)), [VM], parts)
    parts = lax.all_to_all(parts.reshape(8, T, 256), "y", 0, 0)
    act, send = call(
        node_kernel, (shape((T, 256)), shape((8, T + 32, 256))), [VM, VM, VM],
        parts, weight, upstream[0],
    )
    got = lax.all_to_all(send, "y", 0, 0)
    send = call(spread_kernel, shape((4, 8 * T + 16, 256)), [VM], got)
    got = lax.all_to_all(send, "x", 0, 0)
    keep, send, term = call(
        backward_kernel, (shape((8, T, 256)), shape((8 * T + 16, 256)), shape((8, 256), F32)),
        [SM, SM, VM, VM], places, tile_count, tiles, got,
        scratch=[pltpu.VMEM((16, T, 256), F32)],
    )
    got = lax.ppermute(send, "c", swap)
    send = call(join_kernel, shape((8, T + 16, 256)), [VM, VM, VM], keep, got, term)
    got = lax.all_to_all(send, "z", 0, 0)
    grad, term = call(last_kernel, (shape((T, 256)), shape((32, 8, 256), F32)), [VM], got)
    grad_weight = lax.all_to_all(term, ("x", "y"), 0, 0)
    return act[None], grad[None], grad_weight.reshape(256, 256)


def solution(mesh):
    fine = Mesh(mesh.devices.reshape(4, 8, 8, 2), ("x", "y", "z", "c"))
    row, col = ("x", "y"), ("z", "c")
    placed = (
        P(row, col, None),
        P(),
        P(row, col, None, None, None),
        P(row, col, None, None),
        P(row, col),
        P(col, row, None),
    )
    return jax.shard_map(
        per_device,
        mesh=fine,
        in_specs=placed,
        out_specs=(P(col, row, None), P(row, col, None), P()),
        check_vma=False,
    )
```

```python
import jax
import jax.numpy as jnp
from jax import lax
from jax.experimental import pallas as pl
from jax.experimental.pallas import tpu as pltpu
from jax.sharding import Mesh, PartitionSpec as P

BF = jnp.bfloat16
F32 = jnp.float32
VM = pl.BlockSpec(memory_space=pltpu.VMEM)
SM = pl.BlockSpec(memory_space=pltpu.SMEM)
T = 128
GROUP = 4


def call(kernel, outs, in_specs, *args, scratch=(), limit=24 << 20):
    return pl.pallas_call(
        kernel,
        out_shape=outs,
        in_specs=in_specs,
        out_specs=jax.tree.map(lambda _: VM, outs),
        scratch_shapes=scratch,
        compiler_params=pltpu.CompilerParams(vmem_limit_bytes=limit),
    )(*args)


def shape(dims, kind=BF):
    return jax.ShapeDtypeStruct(dims, kind)


def block_products(count_ref, tiles_ref, acc_ref, put, load, contract):
    slots = tiles_ref.shape[0]
    acc_ref[...] = jnp.zeros_like(acc_ref)
    count = count_ref[0, 0]

    def group(g, carry):
        products = []
        for k in range(GROUP):
            s = jnp.minimum(g * GROUP + k, slots - 1)
            product = lax.dot_general(
                tiles_ref[s], load(s), (((contract,), (0,)), ((), ())), preferred_element_type=F32
            )
            products.append((put(s), jnp.where(g * GROUP + k < count, product, 0.0)))
        for at, product in products:
            acc_ref[at] += product
        return carry

    lax.fori_loop(0, (count + GROUP - 1) // GROUP, group, 0)


def forward_kernel(places, count, tiles, own, other, out, acc):
    core = lax.axis_index("c")

    def load(s):
        col = places[1, s]
        z = col // 2
        return jnp.where(col % 2 == core, own[z], other[z])

    block_products(count, tiles, acc, lambda s: places[0, s], load, 1)
    out[...] = acc[...].astype(BF).reshape(out.shape)


def sum_kernel(parts, out):
    total = parts[0].astype(F32)
    for k in range(1, parts.shape[0]):
        total += parts[k].astype(F32)
    out[...] = total.astype(BF)


def node_kernel(parts, weight, upstream, act, send):
    agg = parts[0].astype(F32)
    for k in range(1, parts.shape[0]):
        agg += parts[k].astype(F32)
    agg = agg.astype(BF)
    pre = jnp.dot(agg, weight[...], preferred_element_type=F32)
    sigma = jax.nn.sigmoid(pre)
    act[...] = (pre * sigma).astype(BF)
    slope = (upstream[...].astype(F32) * sigma * (1.0 + pre * (1.0 - sigma))).astype(BF)
    back = lax.dot_general(
        slope, weight[...], (((1,), (1,)), ((), ())), preferred_element_type=F32
    ).astype(BF)
    term = lax.dot_general(agg, slope, (((0,), (0,)), ((), ())), preferred_element_type=F32)
    for y in range(8):
        send[y, :T] = back
        send[y, T:] = term[y * 32 : y * 32 + 32].astype(BF)


def spread_kernel(got, send, term):
    total = got[0, T:].astype(F32)
    for k in range(1, 8):
        total += got[k, T:].astype(F32)
    term[...] = total
    for x in range(4):
        for y in range(8):
            send[x, y * T : (y + 1) * T] = got[y, :T]


def backward_kernel(places, count, tiles, got, keep, send, acc):
    core = lax.axis_index("c")

    def load(s):
        row = places[0, s]
        return got[row // 8, pl.ds(pl.multiple_of((row % 8) * T, T), T)]

    block_products(count, tiles, acc, lambda s: places[1, s], load, 0)
    for z in range(8):
        keep[z] = acc[2 * z + core].astype(BF)
        send[z] = acc[2 * z + 1 - core].astype(BF)


def join_kernel(keep, got, send):
    send[...] = (keep[...].astype(F32) + got[...].astype(F32)).astype(BF)


def gather_kernel(pair, quad, rest, out):
    y = lax.axis_index("y")
    for k in range(2):
        out[y ^ k] = pair[k * 32 : k * 32 + 32]
        out[y ^ (k + 2)] = quad[k * 32 : k * 32 + 32]
    for k in range(4):
        out[y ^ (k + 4)] = rest[k * 32 : k * 32 + 32]


def swap_with(value, axis, bits):
    size = lax.axis_size(axis)
    return lax.ppermute(value, axis, [(i, i ^ bits) for i in range(size)])


def per_device(features, weight, tile_values, tile_places, tile_count, upstream):
    own_rows = features[0]
    tiles = tile_values[0, 0]
    places = tile_places[0, 0]
    swap = [(0, 1), (1, 0)]

    own = lax.all_to_all(jnp.broadcast_to(own_rows, (8, T, 256)), "z", 0, 0)
    other = lax.ppermute(own, "c", swap)
    partial = call(
        forward_kernel, shape((4, 8 * T, 256)), [SM, SM, VM, VM, VM],
        places, tile_count, tiles, own, other, scratch=[pltpu.VMEM((32, T, 256), F32)],
    )
    parts = lax.all_to_all(partial, "x", 0, 0)
    parts = call(sum_kernel, shape((8 * T, 256)), [VM], parts)
    parts = lax.all_to_all(parts.reshape(8, T, 256), "y", 0, 0)
    act, send = call(
        node_kernel, (shape((T, 256)), shape((8, T + 32, 256))), [VM, VM, VM],
        parts, weight, upstream[0],
    )
    got = lax.all_to_all(send, "y", 0, 0)
    send, term = call(
        spread_kernel, (shape((4, 8 * T, 256)), shape((32, 256), F32)), [VM], got
    )
    got = lax.all_to_all(send, "x", 0, 0)
    for axis, bits in (("x", 1), ("x", 3), ("c", 1), ("z", 1), ("z", 2), ("z", 4)):
        term = term + swap_with(term, axis, bits)
    keep, send = call(
        backward_kernel, (shape((8, T, 256)), shape((8, T, 256))), [SM, SM, VM, VM],
        places, tile_count, tiles, got, scratch=[pltpu.VMEM((16, T, 256), F32)],
    )
    got = lax.ppermute(send, "c", swap)
    send = call(join_kernel, shape((8, T, 256)), [VM, VM], keep, got)
    got = lax.all_to_all(send, "z", 0, 0)
    pair = jnp.concatenate([term, swap_with(term, "y", 1)], 0)
    quad = swap_with(pair, "y", 2)
    rest = swap_with(jnp.concatenate([pair, quad], 0), "y", 4)
    grad_weight = call(gather_kernel, shape((8, 32, 256), F32), [VM, VM, VM], pair, quad, rest)
    grad = call(sum_kernel, shape((T, 256)), [VM], got)
    return act[None], grad[None], grad_weight.reshape(256, 256)


def solution(mesh):
    fine = Mesh(mesh.devices.reshape(4, 8, 8, 2), ("x", "y", "z", "c"))
    row, col = ("x", "y"), ("z", "c")
    placed = (
        P(row, col, None),
        P(),
        P(row, col, None, None, None),
        P(row, col, None, None),
        P(row, col),
        P(col, row, None),
    )
    return jax.shard_map(
        per_device,
        mesh=fine,
        in_specs=placed,
        out_specs=(P(col, row, None), P(row, col, None), P()),
        check_vma=False,
    )
```

```python
import jax
import jax.numpy as jnp
from jax import lax
from jax.experimental import pallas as pl
from jax.experimental.pallas import tpu as pltpu
from jax.sharding import Mesh, PartitionSpec as P

BF = jnp.bfloat16
F32 = jnp.float32
VM = pl.BlockSpec(memory_space=pltpu.VMEM)
SM = pl.BlockSpec(memory_space=pltpu.SMEM)
T = 128
GROUP = 4


def call(kernel, outs, in_specs, *args, scratch=(), limit=24 << 20):
    return pl.pallas_call(
        kernel,
        out_shape=outs,
        in_specs=in_specs,
        out_specs=jax.tree.map(lambda _: VM, outs),
        scratch_shapes=scratch,
        compiler_params=pltpu.CompilerParams(vmem_limit_bytes=limit),
    )(*args)


def shape(dims, kind=BF):
    return jax.ShapeDtypeStruct(dims, kind)


def block_products(count_ref, tiles_ref, acc_ref, put, load, contract):
    slots = tiles_ref.shape[0]
    acc_ref[...] = jnp.zeros_like(acc_ref)
    count = count_ref[0, 0]

    def group(g, carry):
        products = []
        for k in range(GROUP):
            s = jnp.minimum(g * GROUP + k, slots - 1)
            product = lax.dot_general(
                tiles_ref[s], load(s), (((contract,), (0,)), ((), ())), preferred_element_type=F32
            )
            products.append((put(s), jnp.where(g * GROUP + k < count, product, 0.0)))
        for at, product in products:
            acc_ref[at] += product
        return carry

    lax.fori_loop(0, (count + GROUP - 1) // GROUP, group, 0)


def forward_kernel(places, count, tiles, own, other, out, acc):
    core = lax.axis_index("c")

    def load(s):
        col = places[1, s]
        z = col // 2
        return jnp.where(col % 2 == core, own[z], other[z])

    block_products(count, tiles, acc, lambda s: places[0, s], load, 1)
    for row in range(32):
        at = (row % 8) // 2 * T
        out[row // 8 * 2 + row % 2, at : at + T] = acc[row].astype(BF)


def sum_kernel(parts, out):
    total = parts[0].astype(F32)
    for k in range(1, parts.shape[0]):
        total += parts[k].astype(F32)
    out[...] = total.astype(BF)


def node_kernel(parts, weight, upstream, act, send):
    agg = parts[0].astype(F32)
    for k in range(1, parts.shape[0]):
        agg += parts[k].astype(F32)
    agg = agg.astype(BF)
    pre = jnp.dot(agg, weight[...], preferred_element_type=F32)
    sigma = jax.nn.sigmoid(pre)
    act[...] = (pre * sigma).astype(BF)
    slope = (upstream[...].astype(F32) * sigma * (1.0 + pre * (1.0 - sigma))).astype(BF)
    back = lax.dot_general(
        slope, weight[...], (((1,), (1,)), ((), ())), preferred_element_type=F32
    ).astype(BF)
    term = lax.dot_general(agg, slope, (((0,), (0,)), ((), ())), preferred_element_type=F32)
    for h in range(4):
        send[h, :T] = back
        for x in range(4):
            at = x * 64 + h * 16
            send[h, T + x * 16 : T + x * 16 + 16] = term[at : at + 16].astype(BF)


def spread_kernel(got, send):
    term = got[0, T:].astype(F32)
    for k in range(1, 4):
        term += got[k, T:].astype(F32)
    high = term.astype(BF).astype(F32)
    low = term - high
    for k in range(8):
        for h in range(4):
            send[k, h * T : (h + 1) * T] = got[h, :T]
        rows = slice(k * 8, k * 8 + 8)
        send[k, 4 * T :] = jnp.concatenate([high[rows], low[rows]], 0).astype(BF)


def backward_kernel(places, count, tiles, got, keep, send, term, acc):
    core = lax.axis_index("c")

    def load(s):
        row = places[0, s]
        at = (row % 8) // 2 * T
        return got[row // 8 * 2 + row % 2, pl.ds(pl.multiple_of(at, T), T)]

    block_products(count, tiles, acc, lambda s: places[1, s], load, 0)
    for z in range(8):
        keep[z] = acc[2 * z + core].astype(BF)
        send[z * T : (z + 1) * T] = acc[2 * z + 1 - core].astype(BF)
    total = got[0, 4 * T :].astype(F32)
    for k in range(1, 8):
        total += got[k, 4 * T :].astype(F32)
    total = total[:8] + total[8:]
    term[...] = total
    high = total.astype(BF).astype(F32)
    send[8 * T :] = jnp.concatenate([high, total - high], 0).astype(BF)


def join_kernel(keep, got, term, send):
    other = got[8 * T :].astype(F32)
    total = term[...] + (other[:8] + other[8:])
    high = total.astype(BF).astype(F32)
    both = jnp.concatenate([high, total - high], 0).astype(BF)
    for z in range(8):
        send[z, :T] = (keep[z].astype(F32) + got[z * T : (z + 1) * T].astype(F32)).astype(BF)
        send[z, T:] = both


def last_kernel(got, grad, term):
    total = got[0].astype(F32)
    for k in range(1, 8):
        total += got[k].astype(F32)
    grad[...] = total[:T].astype(BF)
    rows = total[T : T + 8] + total[T + 8 :]
    for k in range(32):
        term[k] = rows


def per_device(features, weight, tile_values, tile_places, tile_count, upstream):
    own_rows = features[0]
    tiles = tile_values[0, 0]
    places = tile_places[0, 0]
    swap = [(0, 1), (1, 0)]

    own = lax.all_to_all(jnp.broadcast_to(own_rows, (8, T, 256)), "z", 0, 0)
    other = lax.ppermute(own, "c", swap)
    partial = call(
        forward_kernel, shape((8, 4 * T, 256)), [SM, SM, VM, VM, VM],
        places, tile_count, tiles, own, other, scratch=[pltpu.VMEM((32, T, 256), F32)],
    )
    parts = lax.all_to_all(partial, ("x", "yl"), 0, 0)
    parts = call(sum_kernel, shape((4 * T, 256)), [VM], parts)
    parts = lax.all_to_all(parts.reshape(4, T, 256), "yh", 0, 0)
    act, send = call(
        node_kernel, (shape((T, 256)), shape((4, T + 64, 256))), [VM, VM, VM],
        parts, weight, upstream[0],
    )
    got = lax.all_to_all(send, "yh", 0, 0)
    send = call(spread_kernel, shape((8, 4 * T + 16, 256)), [VM], got)
    got = lax.all_to_all(send, ("x", "yl"), 0, 0)
    keep, send, term = call(
        backward_kernel, (shape((8, T, 256)), shape((8 * T + 16, 256)), shape((8, 256), F32)),
        [SM, SM, VM, VM], places, tile_count, tiles, got,
        scratch=[pltpu.VMEM((16, T, 256), F32)],
    )
    got = lax.ppermute(send, "c", swap)
    send = call(join_kernel, shape((8, T + 16, 256)), [VM, VM, VM], keep, got, term)
    got = lax.all_to_all(send, "z", 0, 0)
    grad, term = call(last_kernel, (shape((T, 256)), shape((32, 8, 256), F32)), [VM], got)
    grad_weight = lax.all_to_all(term, ("x", "yh", "yl"), 0, 0)
    return act[None], grad[None], grad_weight.reshape(256, 256)


def solution(mesh):
    fine = Mesh(mesh.devices.reshape(4, 4, 2, 8, 2), ("x", "yh", "yl", "z", "c"))
    row, col = ("x", "yh", "yl"), ("z", "c")
    placed = (
        P(row, col, None),
        P(),
        P(row, col, None, None, None),
        P(row, col, None, None),
        P(row, col),
        P(col, row, None),
    )
    return jax.shard_map(
        per_device,
        mesh=fine,
        in_specs=placed,
        out_specs=(P(col, row, None), P(row, col, None), P()),
        check_vma=False,
    )
```

```python
import jax
import jax.numpy as jnp
from jax import lax
from jax.experimental import pallas as pl
from jax.experimental.pallas import tpu as pltpu
from jax.sharding import Mesh, PartitionSpec as P

BF = jnp.bfloat16
F32 = jnp.float32
VM = pl.BlockSpec(memory_space=pltpu.VMEM)
SM = pl.BlockSpec(memory_space=pltpu.SMEM)
T = 128
GROUP = 4


def call(kernel, outs, in_specs, *args, scratch=(), limit=24 << 20):
    return pl.pallas_call(
        kernel,
        out_shape=outs,
        in_specs=in_specs,
        out_specs=jax.tree.map(lambda _: VM, outs),
        scratch_shapes=scratch,
        compiler_params=pltpu.CompilerParams(vmem_limit_bytes=limit),
    )(*args)


def shape(dims, kind=BF):
    return jax.ShapeDtypeStruct(dims, kind)


def block_products(count_ref, tiles_ref, acc_ref, put, load, contract):
    slots = tiles_ref.shape[0]
    acc_ref[...] = jnp.zeros_like(acc_ref)
    count = count_ref[0, 0]

    def group(g, carry):
        products = []
        for k in range(GROUP):
            s = jnp.minimum(g * GROUP + k, slots - 1)
            product = lax.dot_general(
                tiles_ref[s], load(s), (((contract,), (0,)), ((), ())), preferred_element_type=F32
            )
            products.append((put(s), jnp.where(g * GROUP + k < count, product, 0.0)))
        for at, product in products:
            acc_ref[at] += product
        return carry

    lax.fori_loop(0, (count + GROUP - 1) // GROUP, group, 0)


def forward_kernel(places, count, tiles, own, other, out, acc):
    core = lax.axis_index("c")

    def load(s):
        col = places[1, s]
        z = col // 2
        return jnp.where(col % 2 == core, own[z], other[z])

    block_products(count, tiles, acc, lambda s: places[0, s], load, 1)
    for row in range(32):
        at = (row % 8) // 2 * T
        out[row // 8 * 2 + row % 2, at : at + T] = acc[row].astype(BF)


def fold_kernel(parts, *outs):
    me = lax.axis_index("yh")
    for k in range(4):
        at = pl.multiple_of((me + k) % 4 * T, T)
        total = parts[0, pl.ds(at, T)].astype(F32)
        for j in range(1, 8):
            total += parts[j, pl.ds(at, T)].astype(F32)
        outs[k][...] = total.astype(BF)


def node_kernel(mine, one, two, three, weight, upstream, act, back, term):
    agg = (mine[...].astype(F32) + one[...].astype(F32)) + (
        two[...].astype(F32) + three[...].astype(F32)
    )
    agg = agg.astype(BF)
    pre = jnp.dot(agg, weight[...], preferred_element_type=F32)
    sigma = jax.nn.sigmoid(pre)
    act[...] = (pre * sigma).astype(BF)
    slope = (upstream[...].astype(F32) * sigma * (1.0 + pre * (1.0 - sigma))).astype(BF)
    back[...] = lax.dot_general(
        slope, weight[...], (((1,), (1,)), ((), ())), preferred_element_type=F32
    ).astype(BF)
    product = lax.dot_general(agg, slope, (((0,), (0,)), ((), ())), preferred_element_type=F32)
    term[...] = product.astype(BF).reshape(8, 32, 256)


def pack_kernel(back, got, send):
    send[:T] = back[...]
    term = got[0].astype(F32)
    for k in range(1, 8):
        term += got[k].astype(F32)
    send[T:] = term.astype(BF)


def spread_kernel(mine, one, two, three, send, terms):
    me = lax.axis_index("yh")
    for k, part in enumerate((mine, one, two, three)):
        h = (me + 4 - k) % 4
        terms[h] = part[T:].astype(F32)
        at = pl.multiple_of(h * T, T)
        for j in range(8):
            send[j, pl.ds(at, T)] = part[:T]
    total = ((terms[0] + terms[1]) + (terms[2] + terms[3])).astype(BF)
    for j in range(8):
        send[j, 4 * T :] = total


def backward_kernel(places, count, tiles, got, keep, send, term, acc):
    core = lax.axis_index("c")

    def load(s):
        row = places[0, s]
        at = (row % 8) // 2 * T
        return got[row // 8 * 2 + row % 2, pl.ds(pl.multiple_of(at, T), T)]

    block_products(count, tiles, acc, lambda s: places[1, s], load, 0)
    for z in range(8):
        keep[z] = acc[2 * z + core].astype(BF)
        send[z * T : (z + 1) * T] = acc[2 * z + 1 - core].astype(BF)
    total = got[0, 4 * T :].astype(F32)
    for k in range(1, 8):
        total += got[k, 4 * T :].astype(F32)
    term[...] = total
    high = total.astype(BF)
    send[8 * T : 8 * T + 32] = high
    send[8 * T + 32 :] = (total - high.astype(F32)).astype(BF)


def join_kernel(keep, got, term, send):
    other = got[8 * T : 8 * T + 32].astype(F32) + got[8 * T + 32 :].astype(F32)
    mine = term[...]
    high = mine.astype(BF).astype(F32)
    mine = high + (mine - high).astype(BF).astype(F32)
    both = (mine + other).astype(BF)
    for z in range(8):
        send[z, :T] = (keep[z].astype(F32) + got[z * T : (z + 1) * T].astype(F32)).astype(BF)
        send[z, T:] = both


def last_kernel(got, grad, term):
    total = got[0, :T].astype(F32)
    for k in range(1, 8):
        total += got[k, :T].astype(F32)
    grad[...] = total.astype(BF)
    for k in range(8):
        term[k * 32 : k * 32 + 32] = got[k, T:].astype(F32)


def shifted(value, by):
    return lax.ppermute(value, "yh", [(i, (i + by) % 4) for i in range(4)])


def per_device(features, weight, tile_values, tile_places, tile_count, upstream):
    own_rows = features[0]
    tiles = tile_values[0, 0]
    places = tile_places[0, 0]
    swap = [(0, 1), (1, 0)]

    own = lax.all_to_all(jnp.broadcast_to(own_rows, (8, T, 256)), "z", 0, 0)
    other = lax.ppermute(own, "c", swap)
    partial = call(
        forward_kernel, shape((8, 4 * T, 256)), [SM, SM, VM, VM, VM],
        places, tile_count, tiles, own, other, scratch=[pltpu.VMEM((32, T, 256), F32)],
    )
    parts = lax.all_to_all(partial, ("x", "yl"), 0, 0)
    parts = call(fold_kernel, (shape((T, 256)),) * 4, [VM], parts)
    parts = [parts[0]] + [shifted(parts[k], k) for k in (1, 2, 3)]
    act, back, term = call(
        node_kernel, (shape((T, 256)), shape((T, 256)), shape((8, 32, 256))), [VM] * 6,
        *parts, weight, upstream[0],
    )
    term = lax.all_to_all(term, "z", 0, 0)
    send = call(pack_kernel, shape((T + 32, 256)), [VM, VM], back, term)
    sends = [send] + [shifted(send, k) for k in (1, 2, 3)]
    send = call(
        spread_kernel, shape((8, 4 * T + 32, 256)), [VM] * 4, *sends,
        scratch=[pltpu.VMEM((4, 32, 256), F32)],
    )
    got = lax.all_to_all(send, ("x", "yl"), 0, 0)
    keep, send, term = call(
        backward_kernel, (shape((8, T, 256)), shape((8 * T + 64, 256)), shape((32, 256), F32)),
        [SM, SM, VM, VM], places, tile_count, tiles, got,
        scratch=[pltpu.VMEM((16, T, 256), F32)],
    )
    got = lax.ppermute(send, "c", swap)
    send = call(join_kernel, shape((8, T + 32, 256)), [VM, VM, VM], keep, got, term)
    got = lax.all_to_all(send, "z", 0, 0)
    grad, grad_weight = call(last_kernel, (shape((T, 256)), shape((256, 256), F32)), [VM], got)
    return act[None], grad[None], grad_weight


def solution(mesh):
    fine = Mesh(mesh.devices.reshape(4, 4, 2, 8, 2), ("x", "yh", "yl", "z", "c"))
    row, col = ("x", "yh", "yl"), ("z", "c")
    placed = (
        P(row, col, None),
        P(),
        P(row, col, None, None, None),
        P(row, col, None, None),
        P(row, col),
        P(col, row, None),
    )
    return jax.shard_map(
        per_device,
        mesh=fine,
        in_specs=placed,
        out_specs=(P(col, row, None), P(row, col, None), P()),
        check_vma=False,
    )
```

```python
import jax
import jax.numpy as jnp
from jax import lax
from jax.experimental import pallas as pl
from jax.experimental.pallas import tpu as pltpu
from jax.sharding import Mesh, PartitionSpec as P

BF = jnp.bfloat16
F32 = jnp.float32
VM = pl.BlockSpec(memory_space=pltpu.VMEM)
SM = pl.BlockSpec(memory_space=pltpu.SMEM)
T = 128
GROUP = 4


def call(kernel, outs, in_specs, *args, scratch=(), limit=24 << 20):
    return pl.pallas_call(
        kernel,
        out_shape=outs,
        in_specs=in_specs,
        out_specs=jax.tree.map(lambda _: VM, outs),
        scratch_shapes=scratch,
        compiler_params=pltpu.CompilerParams(vmem_limit_bytes=limit),
    )(*args)


def shape(dims, kind=BF):
    return jax.ShapeDtypeStruct(dims, kind)


def block_products(count_ref, tiles_ref, acc_ref, put, load, contract):
    slots = tiles_ref.shape[0]
    acc_ref[...] = jnp.zeros_like(acc_ref)
    count = count_ref[0, 0]

    def group(g, carry):
        products = []
        for k in range(GROUP):
            s = jnp.minimum(g * GROUP + k, slots - 1)
            product = lax.dot_general(
                tiles_ref[s], load(s), (((contract,), (0,)), ((), ())), preferred_element_type=F32
            )
            products.append((put(s), jnp.where(g * GROUP + k < count, product, 0.0)))
        for at, product in products:
            acc_ref[at] += product
        return carry

    lax.fori_loop(0, (count + GROUP - 1) // GROUP, group, 0)


def forward_kernel(places, count, tiles, own, other, out, acc):
    core = lax.axis_index("c")

    def load(s):
        col = places[1, s]
        z = col // 2
        return jnp.where(col % 2 == core, own[z], other[z])

    block_products(count, tiles, acc, lambda s: places[0, s], load, 1)
    for row in range(32):
        at = (row % 8) // 2 * T
        out[row // 8 * 2 + row % 2, at : at + T] = acc[row].astype(BF)


def fold_kernel(parts, out):
    total = parts[0].astype(F32)
    for k in range(1, parts.shape[0]):
        total += parts[k].astype(F32)
    out[...] = total.astype(BF)


def node_kernel(parts, weight, upstream, act, back, term):
    agg = parts[0].astype(F32)
    for k in range(1, parts.shape[0]):
        agg += parts[k].astype(F32)
    agg = agg.astype(BF)
    pre = jnp.dot(agg, weight[...], preferred_element_type=F32)
    sigma = jax.nn.sigmoid(pre)
    act[...] = (pre * sigma).astype(BF)
    slope = (upstream[...].astype(F32) * sigma * (1.0 + pre * (1.0 - sigma))).astype(BF)
    back[...] = lax.dot_general(
        slope, weight[...], (((1,), (1,)), ((), ())), preferred_element_type=F32
    ).astype(BF)
    product = lax.dot_general(agg, slope, (((0,), (0,)), ((), ())), preferred_element_type=F32)
    term[...] = product.astype(BF).reshape(8, 32, 256)


def pack_kernel(back, got, send):
    term = got[0].astype(F32)
    for k in range(1, 8):
        term += got[k].astype(F32)
    term = term.astype(BF)
    for h in range(4):
        send[h, :T] = back[...]
        send[h, T:] = term


def spread_kernel(got, send):
    term = got[0, T:].astype(F32)
    for k in range(1, 4):
        term += got[k, T:].astype(F32)
    term = term.astype(BF)
    for j in range(8):
        for h in range(4):
            send[j, h * T : (h + 1) * T] = got[h, :T]
        send[j, 4 * T :] = term


def backward_kernel(places, count, tiles, got, keep, send, term, acc):
    core = lax.axis_index("c")

    def load(s):
        row = places[0, s]
        at = (row % 8) // 2 * T
        return got[row // 8 * 2 + row % 2, pl.ds(pl.multiple_of(at, T), T)]

    block_products(count, tiles, acc, lambda s: places[1, s], load, 0)
    for z in range(8):
        keep[z] = acc[2 * z + core].astype(BF)
        send[z * T : (z + 1) * T] = acc[2 * z + 1 - core].astype(BF)
    total = got[0, 4 * T :].astype(F32)
    for k in range(1, 8):
        total += got[k, 4 * T :].astype(F32)
    term[...] = total
    high = total.astype(BF)
    send[8 * T : 8 * T + 32] = high
    send[8 * T + 32 :] = (total - high.astype(F32)).astype(BF)


def join_kernel(keep, got, term, send):
    other = got[8 * T : 8 * T + 32].astype(F32) + got[8 * T + 32 :].astype(F32)
    mine = term[...]
    high = mine.astype(BF).astype(F32)
    mine = high + (mine - high).astype(BF).astype(F32)
    both = (mine + other).astype(BF)
    for z in range(8):
        send[z, :T] = (keep[z].astype(F32) + got[z * T : (z + 1) * T].astype(F32)).astype(BF)
        send[z, T:] = both


def last_kernel(got, grad, term):
    total = got[0, :T].astype(F32)
    for k in range(1, 8):
        total += got[k, :T].astype(F32)
    grad[...] = total.astype(BF)
    for k in range(8):
        term[k * 32 : k * 32 + 32] = got[k, T:].astype(F32)


def per_device(features, weight, tile_values, tile_places, tile_count, upstream):
    own_rows = features[0]
    tiles = tile_values[0, 0]
    places = tile_places[0, 0]
    swap = [(0, 1), (1, 0)]

    own = lax.all_to_all(jnp.broadcast_to(own_rows, (8, T, 256)), "z", 0, 0)
    other = lax.ppermute(own, "c", swap)
    partial = call(
        forward_kernel, shape((8, 4 * T, 256)), [SM, SM, VM, VM, VM],
        places, tile_count, tiles, own, other, scratch=[pltpu.VMEM((32, T, 256), F32)],
    )
    parts = lax.all_to_all(partial, ("x", "yl"), 0, 0)
    parts = call(fold_kernel, shape((4 * T, 256)), [VM], parts)
    parts = lax.all_to_all(parts.reshape(4, T, 256), "yh", 0, 0)
    act, back, term = call(
        node_kernel, (shape((T, 256)), shape((T, 256)), shape((8, 32, 256))), [VM] * 3,
        parts, weight, upstream[0],
    )
    term = lax.all_to_all(term, "z", 0, 0)
    send = call(pack_kernel, shape((4, T + 32, 256)), [VM, VM], back, term)
    got = lax.all_to_all(send, "yh", 0, 0)
    send = call(spread_kernel, shape((8, 4 * T + 32, 256)), [VM], got)
    got = lax.all_to_all(send, ("x", "yl"), 0, 0)
    keep, send, term = call(
        backward_kernel, (shape((8, T, 256)), shape((8 * T + 64, 256)), shape((32, 256), F32)),
        [SM, SM, VM, VM], places, tile_count, tiles, got,
        scratch=[pltpu.VMEM((16, T, 256), F32)],
    )
    got = lax.ppermute(send, "c", swap)
    send = call(join_kernel, shape((8, T + 32, 256)), [VM, VM, VM], keep, got, term)
    got = lax.all_to_all(send, "z", 0, 0)
    grad, grad_weight = call(last_kernel, (shape((T, 256)), shape((256, 256), F32)), [VM], got)
    return act[None], grad[None], grad_weight


def solution(mesh):
    fine = Mesh(mesh.devices.reshape(4, 4, 2, 8, 2), ("x", "yh", "yl", "z", "c"))
    row, col = ("x", "yh", "yl"), ("z", "c")
    placed = (
        P(row, col, None),
        P(),
        P(row, col, None, None, None),
        P(row, col, None, None),
        P(row, col),
        P(col, row, None),
    )
    return jax.shard_map(
        per_device,
        mesh=fine,
        in_specs=placed,
        out_specs=(P(col, row, None), P(row, col, None), P()),
        check_vma=False,
    )
```
